512 devices in a mesh: shot: 32 (over z, x), depth: 16 (over y, core).
Axes of the slice: x: 4, y: 8, z: 8, core: 2. Of those that a mesh axis runs over, the one named last changes fastest.
Arguments:
- prev_fields: float32 [32, 2, 128, 64, 128], P('shot', None, 'depth'), may hold values from -6 to 6
- cur_fields: float32 [32, 2, 128, 64, 128], P('shot', None, 'depth'), may hold values from -6 to 6
- speed_term: bfloat16 [32, 128, 64, 128], P('shot', 'depth'), may hold values from 0.039794922 to 0.119628906
- epsilon: bfloat16 [32, 128, 64, 128], P('shot', 'depth'), may hold values from 0 to 0.25
- tilt: bfloat16 [32, 128, 64, 128], P('shot', 'depth'), may hold values from 0 to 1.5
- azimuth: bfloat16 [32, 128, 64, 128], P('shot', 'depth'), may hold values from -3.140625 to 3.140625
- aperture_anchor: int32 [32], replicated, may hold values from -32 to 96
- slot_block: int32 [128], replicated, may hold values from 0 to 127, as said below
- band_width: int32 [128], replicated, may hold values from 1 to 4
- depth_damp: float32 [128], replicated, may hold values from 0.02 to 0.1
Outputs:
- gradient: float32 [128, 128, 128], P('shot', 'depth')
The draws below stay inside these ranges and needn't reach their ends.
Inputs may be any that keep to these rules, and one draw needn't show every extreme that they name: Slots 4 * q to 4 * q + 3 hold the image blocks 2 r, 2 r + 1, 2 r + 64 and 2 r + 128 / 2 + 1 for some r, each r once, so that slot_block is a permutation of the blocks. `aperture_anchor`: every aperture covers at least 32 image blocks, and at most 2 of them held by one shot index; every aperture reaches 2 for some shot index.
All inputs are finite; a program needn't handle non-finite values.
Results may differ from the reference program's by a relative error of at most 0.0003.
Values may be sent and summed in bfloat16 or wider, within the bound.
No kernel may reach another device: no remote copies, remote signals or barrier semaphores. Data moves between devices by JAX's collectives and lax.ppermute only.
A program may use at most 64 MiB of HBM per device.

```python
import math
import jax
import jax.numpy as jnp
from jax import lax

AY = 128
NT = 8
WMAX = 4
SHOTS = 32
NB = 128
AX = 64
NZ = 128


def draw_slot_block(key, part):
    holders = NB // 4
    order = jax.random.permutation(key, holders)
    first = 2 * order
    middle = NB // 2
    blocks = jnp.stack([first, first + 1, first + middle, first + middle + 1], axis=1)
    return blocks.reshape(NB).astype(jnp.int32)


def set_ends(values, own_key, least, top_value):
    spot = [jax.random.randint(jax.random.fold_in(own_key, axis), (), 0, length) for axis, length in enumerate(values.shape)]
    longest = values.shape.index(max(values.shape))
    beside = spot[:longest] + [(spot[longest] + 1) % values.shape[longest]] + spot[longest + 1:]
    return values.at[tuple(spot)].set(least).at[tuple(beside)].set(top_value)


def steps_of(stream_key, dims, shards, smallest, largest):
    gain = 1.0
    for position, blocks in shards:
        draws = jax.random.uniform(jax.random.fold_in(jax.random.fold_in(stream_key, 6), position), (blocks,), jnp.float32, smallest / len(shards), largest / len(shards))
        gain = gain * jnp.repeat(jnp.exp(draws), dims[position] // blocks).reshape((-1,) + (1,) * (len(dims) - 1 - position))
    return gain


def gaussian(rng, shape, width, limit, split=(), held_as=jnp.bfloat16):
    array = jax.random.normal(rng, shape, jnp.float32) * width
    if len(split) > 0:
        array = steps_of(rng, shape, split, -0.22, 0.18) * array
    return jnp.clip(array, min=-limit, max=limit).astype(held_as)


def setup_inputs(seed: int = 0) -> dict:
    key_of = jax.random.split(jax.random.key(seed), 11)
    prev_fields = gaussian(key_of[0], (SHOTS, 2, NZ, AX, AY), 1.0, 6.0, ((0, 32), (2, 16)), jnp.float32)
    cur_fields = gaussian(key_of[1], (SHOTS, 2, NZ, AX, AY), 1.0, 6.0, ((0, 32), (2, 16)), jnp.float32)
    speed_term = jnp.clip(0.039794922 + 0.079833984 * jax.random.uniform(key_of[2], (SHOTS, NZ, AX, AY), jnp.float32) ** steps_of(key_of[2], (SHOTS, NZ, AX, AY), ((0, 32), (1, 16)), -0.2, 0.2), 0.039794922, 0.119628906).astype(jnp.bfloat16)
    epsilon = jnp.clip(0.25 * jax.random.uniform(key_of[3], (SHOTS, NZ, AX, AY), jnp.float32) ** steps_of(key_of[3], (SHOTS, NZ, AX, AY), ((0, 32), (1, 16)), -0.2, 0.2), 0.0, 0.25).astype(jnp.bfloat16)
    tilt = jnp.clip(1.5 * jax.random.uniform(key_of[4], (SHOTS, NZ, AX, AY), jnp.float32) ** steps_of(key_of[4], (SHOTS, NZ, AX, AY), ((0, 32), (1, 16)), -0.2, 0.2), 0.0, 1.5).astype(jnp.bfloat16)
    azimuth = jnp.clip(jax.random.uniform(key_of[5], (SHOTS, NZ, AX, AY), jnp.float32, -3.140625, 3.140625), -3.140625, 3.140625).astype(jnp.bfloat16)
    aperture_anchor = set_ends(jax.random.randint(key_of[6], (SHOTS,), 0 - AX // 2, NB - AX // 2 + 1), jax.random.fold_in(key_of[6], 1), 0 - AX // 2, (NB - AX // 2 + 1) - 1).astype(jnp.int32)
    slot_block = draw_slot_block(jax.random.fold_in(key_of[10], 71), 0)
    band_width = set_ends(jax.random.randint(key_of[8], (NZ,), 1, WMAX + 1), jax.random.fold_in(key_of[8], 1), 1, WMAX).astype(jnp.int32)
    depth_damp = jnp.clip(jnp.exp(jax.random.uniform(key_of[9], (NZ,), jnp.float32, math.log(0.02), math.log(0.1))), 0.02, 0.1)
    return {"prev_fields": prev_fields, "cur_fields": cur_fields, "speed_term": speed_term, "epsilon": epsilon, "tilt": tilt, "azimuth": azimuth, "aperture_anchor": aperture_anchor, "slot_block": slot_block, "band_width": band_width, "depth_damp": depth_damp}


def weights_of(speed_term, epsilon, tilt, azimuth):
    speed = speed_term.astype(jnp.float32)
    ratio = epsilon.astype(jnp.float32)
    theta = tilt.astype(jnp.float32)
    sweep = azimuth.astype(jnp.float32)
    sine = jnp.sin(theta)
    axis_z = jnp.cos(theta)
    axis_x = sine * jnp.cos(sweep)
    axis_y = sine * jnp.sin(sweep)
    iso_part = 1.0 + 2.0 * ratio
    anisotropy = -2.0 * ratio
    return (speed * (iso_part + anisotropy * axis_z * axis_z), speed * (iso_part + anisotropy * axis_x * axis_x), speed * (iso_part + anisotropy * axis_y * axis_y), speed * (2.0 * anisotropy * axis_z * axis_x), speed * (2.0 * anisotropy * axis_z * axis_y), speed * (2.0 * anisotropy * axis_x * axis_y))

def apply_operator(extended, weights):
    leading = extended.ndim - 3
    padded = jnp.pad(extended, [(0, 0)] * leading + [(0, 0), (1, 1), (1, 1)])
    center = padded[..., 1:-1, 1:-1, 1:-1]
    along_z = padded[..., 2:, 1:-1, 1:-1] + padded[..., :-2, 1:-1, 1:-1] - 2.0 * center
    along_x = padded[..., 1:-1, 2:, 1:-1] + padded[..., 1:-1, :-2, 1:-1] - 2.0 * center
    along_y = padded[..., 1:-1, 1:-1, 2:] + padded[..., 1:-1, 1:-1, :-2] - 2.0 * center
    cross_zx = 0.25 * (padded[..., 2:, 2:, 1:-1] - padded[..., 2:, :-2, 1:-1] - padded[..., :-2, 2:, 1:-1] + padded[..., :-2, :-2, 1:-1])
    cross_zy = 0.25 * (padded[..., 2:, 1:-1, 2:] - padded[..., 2:, 1:-1, :-2] - padded[..., :-2, 1:-1, 2:] + padded[..., :-2, 1:-1, :-2])
    cross_xy = 0.25 * (padded[..., 1:-1, 2:, 2:] - padded[..., 1:-1, 2:, :-2] - padded[..., 1:-1, :-2, 2:] + padded[..., 1:-1, :-2, :-2])
    return weights[0] * along_z + weights[1] * along_x + weights[2] * along_y + weights[3] * cross_zx + weights[4] * cross_zy + weights[5] * cross_xy

def band_matrix(band_width, depth_damp):
    length = band_width.shape[0]
    index = jnp.arange(length, dtype=jnp.int32)
    distance = jnp.abs(index[:, None] - index[None, :])
    reach = jnp.maximum(band_width[:, None], band_width[None, :])
    adjacent = ((distance > 0) & (distance <= reach)).astype(jnp.float32)
    return jnp.diag(depth_damp.astype(jnp.float32) + jnp.sum(adjacent, axis=1)) - adjacent

def reference(prev_fields, cur_fields, speed_term, epsilon, tilt, azimuth, aperture_anchor, slot_block, band_width, depth_damp):

    def one_shot(total, shot_index):
        earlier_field = prev_fields[shot_index]
        current = cur_fields[shot_index]
        weights = weights_of(speed_term[shot_index], epsilon[shot_index], tilt[shot_index], azimuth[shot_index])
        picture = jnp.zeros(current.shape[1:], jnp.float32)
        for counter in range(NT):
            extended = jnp.pad(current, ((0, 0), (1, 1), (0, 0), (0, 0)))
            following = 2.0 * current - earlier_field + apply_operator(extended, weights)
            picture = picture + following[0] * following[1]
            earlier_field, current = (current, following)
        picture = picture * (1.0 / NT)
        placed = jnp.transpose(picture, (1, 0, 2))
        start = (aperture_anchor[shot_index] + AX).astype(jnp.int32)
        window = lax.dynamic_slice_in_dim(total, start, AX, 0)
        total = lax.dynamic_update_slice_in_dim(total, window + placed, start, 0)
        return (total, None)
    total = jnp.zeros((NB + 2 * AX, NZ, AY), jnp.float32)
    total, unused = lax.scan(one_shot, total, jnp.arange(SHOTS, dtype=jnp.int32))
    image = total[AX:AX + NB]
    owned = image[slot_block]
    traces = jnp.transpose(owned, (0, 2, 1)).reshape(NB * AY, NZ)
    matrix = band_matrix(band_width, depth_damp)
    solved = jnp.linalg.solve(matrix, traces.T)
    return solved.T.reshape(NB, AY, NZ)
```

```python
import jax
import jax.numpy as jnp
from jax import lax
from jax.experimental import pallas as pl
from jax.experimental.pallas import tpu as pltpu
from jax.sharding import PartitionSpec as P

NT = 8
W = 8
SLAB = 8
EXT = SLAB + 2 * W
AX = 64
AY = 128
PAD = 8


def trig(angle):
    square = angle * angle
    sine = -1.0 / 39916800.0
    for term in (1.0 / 362880.0, -1.0 / 5040.0, 1.0 / 120.0, -1.0 / 6.0, 1.0):
        sine = sine * square + term
    cosine = 1.0 / 479001600.0
    for term in (-1.0 / 3628800.0, 1.0 / 40320.0, -1.0 / 720.0, 1.0 / 24.0, -0.5, 1.0):
        cosine = cosine * square + term
    return sine * angle, cosine


def weight_planes(speed, ratio, theta, sweep):
    sine, axis_z = trig(theta)
    half_sine, half_cosine = trig(0.5 * sweep)
    axis_x = sine * (1.0 - 2.0 * half_sine * half_sine)
    axis_y = sine * (2.0 * half_sine * half_cosine)
    tilted = -2.0 * ratio
    base = speed * (1.0 + 2.0 * ratio)
    tilted = speed * tilted
    cross = 0.5 * tilted
    zz = base + tilted * axis_z * axis_z
    xx = base + tilted * axis_x * axis_x
    yy = base + tilted * axis_y * axis_y
    zx = cross * axis_z * axis_x
    zy = cross * axis_z * axis_y
    xy = cross * axis_x * axis_y
    centre = 2.0 - 2.0 * (zz + xx + yy)
    lane = lax.broadcasted_iota(jnp.int32, speed.shape, 1)
    low = lane == 0
    high = lane == AY - 1

    def up(plane):
        return jnp.where(high, 0.0, pltpu.roll(plane, AY - 1, 1))

    def down(plane):
        return jnp.where(low, 0.0, pltpu.roll(plane, 1, 1))

    return (centre, zz, xx, zx, up(yy), up(-zy), up(-xy), down(yy), down(zy), down(xy))


def stencil_kernel(
    edge, source, cur, prev, speed, ratio, tilt, azimuth,
    cur_low, prev_low, media_low, cur_high, prev_high, media_high,
    send, first, second, planes, picture, *, rows=16, unroll=1,
):
    low_scale = edge[0]
    high_scale = edge[1]
    zeros = jnp.zeros((PAD, AY), jnp.float32)

    body = pl.ds(PAD, AX)
    for field in range(2):
        def clear(layer, carry):
            for buffer in (first, second):
                buffer[field, layer, 0:PAD, :] = zeros
                buffer[field, layer, PAD + AX : PAD + AX + PAD, :] = zeros
            return carry
        lax.fori_loop(0, EXT, clear, 0)

        def load(layer, carry):
            first[field, layer, body, :] = cur_low[field, layer] * low_scale
            first[field, layer + W, body, :] = cur[field, layer]
            first[field, layer + W + SLAB, body, :] = cur_high[field, layer] * high_scale
            second[field, layer + W, body, :] = prev[field, layer]
            return carry
        lax.fori_loop(0, SLAB, load, 0)

        def load_prev(layer, carry):
            second[field, layer + 1, body, :] = prev_low[field, layer] * low_scale
            second[field, layer + W + SLAB, body, :] = prev_high[field, layer] * high_scale
            return carry
        lax.fori_loop(0, W - 1, load_prev, 0)

    def store_planes(layer, speed_part, ratio_part, tilt_part, azimuth_part, scale):
        for start in range(0, AX, 16):
            part = slice(start, start + 16)
            values = weight_planes(
                speed_part[part].astype(jnp.float32) * scale,
                ratio_part[part].astype(jnp.float32),
                tilt_part[part].astype(jnp.float32),
                azimuth_part[part].astype(jnp.float32),
            )
            for index, value in enumerate(values):
                planes[index, layer, part, :] = value

    def own_planes(layer, carry):
        store_planes(layer + W - 1, speed.at[layer], ratio.at[layer], tilt.at[layer], azimuth.at[layer], 1.0)
        return carry

    lax.fori_loop(0, SLAB, own_planes, 0)

    def halo_planes(layer, carry):
        store_planes(layer, *[media_low.at[i, layer] for i in range(4)], low_scale)
        store_planes(layer + W - 1 + SLAB, *[media_high.at[i, layer] for i in range(4)], high_scale)
        return carry

    lax.fori_loop(0, W - 1, halo_planes, 0)

    def advance(source_buffer, target, layer, start):
        part = slice(start, start + rows)
        (centre_w, zz, xx, zx, y_low, zy_low, xy_low, y_high, zy_high, xy_high) = [
            planes[i, layer - 1, part, :] for i in range(10)
        ]
        here = slice(PAD + start, PAD + start + rows)
        before = slice(PAD + start - 1, PAD + start + rows - 1)
        after = slice(PAD + start + 1, PAD + start + rows + 1)
        made = []
        for field in range(2):
            centre = source_buffer[field, layer, here, :]
            above = source_buffer[field, layer + 1, here, :]
            below = source_buffer[field, layer - 1, here, :]
            ahead = source_buffer[field, layer, after, :]
            behind = source_buffer[field, layer, before, :]
            step_z = above - below
            step_x = ahead - behind
            twist = (source_buffer[field, layer + 1, after, :] - source_buffer[field, layer + 1, before, :]) - (
                source_buffer[field, layer - 1, after, :] - source_buffer[field, layer - 1, before, :]
            )
            total = centre_w * centre - target[field, layer, here, :]
            total = total + zz * (above + below)
            total = total + xx * (ahead + behind)
            total = total + zx * twist
            total = total + pltpu.roll(y_low * centre + zy_low * step_z + xy_low * step_x, 1, 1)
            total = total + pltpu.roll(y_high * centre + zy_high * step_z + xy_high * step_x, AY - 1, 1)
            target[field, layer, here, :] = total
            made.append(total)
        return made

    for step in range(1, NT + 1):
        source_buffer, target = (first, second) if step % 2 else (second, first)

        def halo(layer, carry):
            for start in range(0, AX, rows):
                advance(source_buffer, target, layer, start)
            return carry

        def own(layer, carry):
            for start in range(0, AX, rows):
                made = advance(source_buffer, target, layer + W, start)
                place = pl.ds(pl.multiple_of(layer * AX + start, rows), rows)
                product = made[0] * made[1]
                picture[place, :] = product if step == 1 else picture[place, :] + product
            return carry

        if step < NT:
            lax.fori_loop(step, W, halo, 0, unroll=unroll)
        lax.fori_loop(0, SLAB, own, 0, unroll=unroll)
        if step < NT:
            lax.fori_loop(W + SLAB, EXT - step, halo, 0, unroll=unroll)

    for entry in range(source.shape[0]):
        send[entry] = picture[pl.ds(source[entry], SLAB, stride=AX), :]


def stencil(edge, source, cur, prev, speed, ratio, tilt, azimuth, lows, highs):
    vm = pl.BlockSpec(memory_space=pltpu.VMEM)
    sm = pl.BlockSpec(memory_space=pltpu.SMEM)
    n = source.shape[0]
    return pl.pallas_call(
        stencil_kernel,
        out_shape=jax.ShapeDtypeStruct((n, SLAB, AY), jnp.float32),
        in_specs=[sm, sm] + [vm] * 12,
        out_specs=vm,
        scratch_shapes=[
            pltpu.VMEM((2, EXT, AX + 2 * PAD, AY), jnp.float32),
            pltpu.VMEM((2, EXT, AX + 2 * PAD, AY), jnp.float32),
            pltpu.VMEM((10, EXT - 2, AX, AY), jnp.float32),
            pltpu.VMEM((SLAB * AX, AY), jnp.float32),
        ],
    )(edge, source, cur, prev, speed, ratio, tilt, azimuth, *lows, *highs)


VM = pl.BlockSpec(memory_space=pltpu.VMEM)
SM = pl.BlockSpec(memory_space=pltpu.SMEM)
DOUBLINGS = 14


def inverse_kernel(jump, column_scale, inverse, stack):
    size = jump.shape[0]
    row = lax.broadcasted_iota(jnp.int32, (size, size), 0)
    column = lax.broadcasted_iota(jnp.int32, (size, size), 1)
    stack[0:size, :] = (row == column).astype(jnp.float32)
    stack[size : 2 * size, :] = jump[...]

    def double(counter, carry):
        grown = lax.dot_general(
            stack[...], stack[size : 2 * size, :], (((1,), (0,)), ((), ())),
            precision=lax.Precision.HIGHEST, preferred_element_type=jnp.float32,
        )
        stack[0:size, :] = stack[0:size, :] + grown[:size]
        stack[size : 2 * size, :] = grown[size:]
        return carry

    lax.fori_loop(0, DOUBLINGS, double, 0)
    inverse[...] = stack[0:size, :] * column_scale[...]


def band_inverse(band_width, depth_damp):
    length = band_width.shape[0]
    index = jnp.arange(length, dtype=jnp.int32)
    distance = jnp.abs(index[:, None] - index[None, :])
    reach = jnp.maximum(band_width[:, None], band_width[None, :])
    adjacent = ((distance > 0) & (distance <= reach)).astype(jnp.float32)
    diagonal = depth_damp + jnp.sum(adjacent, axis=1)
    scale = 1.0 / diagonal
    return pl.pallas_call(
        inverse_kernel,
        out_shape=jax.ShapeDtypeStruct((length, length), jnp.float32),
        in_specs=[VM, VM],
        out_specs=VM,
        scratch_shapes=[pltpu.VMEM((2 * length, length), jnp.float32)],
    )(adjacent * scale[:, None], scale[None, :])


def gather_kernel(place, rows_in, out, held):
    for slot in range(held.shape[0]):
        held[slot] = jnp.zeros((SLAB, AY), jnp.float32)
    for entry in range(rows_in.shape[0]):
        slot = place[entry]
        held[slot] = held[slot] + rows_in[entry]
    slots = held.shape[0] - 1
    part = AY // out.shape[0]
    lane = lax.broadcasted_iota(jnp.int32, (SLAB, AY), 1)
    for piece in range(out.shape[0]):
        mixed = None
        for slot in range(slots):
            moved = held[slot]
            turn = (slot * part - piece * part) % AY
            if turn:
                moved = pltpu.roll(moved, turn, 1)
            mixed = moved if mixed is None else jnp.where(lane >= slot * part, moved, mixed)
        out[piece] = mixed * (1.0 / NT)


def apply_kernel(inverse, columns, out):
    solved = lax.dot_general(
        columns[...], inverse[...], (((0,), (1,)), ((), ())),
        precision=lax.Precision.HIGHEST, preferred_element_type=jnp.float32,
    )
    slots, part = out.shape[:2]
    for slot in range(slots):
        out[slot] = solved[slot * part : (slot + 1) * part]


def pick_rows(blocks, anchors):
    row = blocks - anchors
    valid = (row >= 0) & (row < AX)
    order = jnp.cumsum(valid.astype(jnp.int32), axis=1) - 1
    return row, valid, order


def shards(
    prev_fields, cur_fields, speed_term, epsilon, tilt, azimuth,
    aperture_anchor, slot_block, band_width, depth_damp,
):
    depth = lax.axis_size("depth")
    shots = lax.axis_size("shot")
    upward = [(i, (i + 1) % depth) for i in range(depth)]
    downward = [((i + 1) % depth, i) for i in range(depth)]
    prev, cur = prev_fields[0], cur_fields[0]
    media = [speed_term[0], epsilon[0], tilt[0], azimuth[0]]
    media_tail = jnp.stack([part[1:] for part in media])
    media_head = jnp.stack([part[: W - 1] for part in media])
    cur_low = lax.ppermute(cur, "depth", upward)
    cur_high = lax.ppermute(cur, "depth", downward)
    lows = (cur_low, lax.ppermute(prev[:, 1:], "depth", upward), lax.ppermute(media_tail, "depth", upward))
    highs = (
        cur_high,
        lax.ppermute(prev[:, : W - 1], "depth", downward),
        lax.ppermute(media_head, "depth", downward),
    )
    my_depth = lax.axis_index("depth")
    my_shot = lax.axis_index("shot")
    edge = jnp.stack([my_depth > 0, my_depth < depth - 1]).astype(jnp.float32)

    held = slot_block.shape[0] // shots
    blocks = slot_block.reshape(shots, held)
    row, valid, order = pick_rows(blocks, aperture_anchor[my_shot])
    source = jnp.stack(
        [jnp.sum(jnp.where(valid & (order == j), row, 0), axis=1) for j in range(2)], axis=1
    ).reshape(-1)
    mine = lax.dynamic_slice_in_dim(slot_block, my_shot * held, held)
    row, valid, order = pick_rows(mine[None, :], aperture_anchor[:, None])
    slot = jnp.arange(held, dtype=jnp.int32)[None, :]
    place = jnp.stack(
        [held + jnp.sum(jnp.where(valid & (order == j), slot - held, 0), axis=1) for j in range(2)], axis=1
    ).reshape(-1)
    inverse = band_inverse(band_width, depth_damp)

    send = stencil(edge, source, cur, prev, *media, lows, highs)
    received = lax.all_to_all(send, "shot", split_axis=0, concat_axis=0, tiled=True)
    part = AY // depth
    pieces = pl.pallas_call(
        gather_kernel,
        out_shape=jax.ShapeDtypeStruct((depth, SLAB, AY), jnp.float32),
        in_specs=[SM, VM],
        out_specs=VM,
        scratch_shapes=[pltpu.VMEM((held + 1, SLAB, AY), jnp.float32)],
    )(place, received)
    columns = lax.all_to_all(pieces, "depth", split_axis=0, concat_axis=0, tiled=True)
    return pl.pallas_call(
        apply_kernel,
        out_shape=jax.ShapeDtypeStruct((held, part, AY), jnp.float32),
        in_specs=[VM, VM],
        out_specs=VM,
    )(inverse, columns.reshape(AY, AY))


def solution(mesh):
    placed = (
        P("shot", None, "depth", None, None),
        P("shot", None, "depth", None, None),
        P("shot", "depth", None, None),
        P("shot", "depth", None, None),
        P("shot", "depth", None, None),
        P("shot", "depth", None, None),
        P(),
        P(),
        P(),
        P(),
    )
    return jax.shard_map(
        shards, mesh=mesh, in_specs=placed, out_specs=P("shot", "depth", None), check_vma=False
    )
```

```python
import jax
import jax.numpy as jnp
from jax import lax
from jax.experimental import pallas as pl
from jax.experimental.pallas import tpu as pltpu
from jax.sharding import PartitionSpec as P

NT = 8
W = 8
SLAB = 8
EXT = SLAB + 2 * W
AX = 64
AY = 128
PAD = 8
NEAR = 4
ROWS = 16
BODY = slice(PAD, PAD + AX)


def trig(angle):
    square = angle * angle
    sine = -1.0 / 39916800.0
    for term in (1.0 / 362880.0, -1.0 / 5040.0, 1.0 / 120.0, -1.0 / 6.0, 1.0):
        sine = sine * square + term
    cosine = 1.0 / 479001600.0
    for term in (-1.0 / 3628800.0, 1.0 / 40320.0, -1.0 / 720.0, 1.0 / 24.0, -0.5, 1.0):
        cosine = cosine * square + term
    return sine * angle, cosine


def weight_planes(speed, ratio, theta, sweep):
    sine, axis_z = trig(theta)
    half_sine, half_cosine = trig(0.5 * sweep)
    axis_x = sine * (1.0 - 2.0 * half_sine * half_sine)
    axis_y = sine * (2.0 * half_sine * half_cosine)
    tilted = -2.0 * ratio
    base = speed * (1.0 + 2.0 * ratio)
    tilted = speed * tilted
    cross = 0.5 * tilted
    zz = base + tilted * axis_z * axis_z
    xx = base + tilted * axis_x * axis_x
    yy = base + tilted * axis_y * axis_y
    zx = cross * axis_z * axis_x
    zy = cross * axis_z * axis_y
    xy = cross * axis_x * axis_y
    centre = 2.0 - 2.0 * (zz + xx + yy)
    lane = lax.broadcasted_iota(jnp.int32, speed.shape, 1)
    low = lane == 0
    high = lane == AY - 1

    def up(plane):
        return jnp.where(high, 0.0, pltpu.roll(plane, AY - 1, 1))

    def down(plane):
        return jnp.where(low, 0.0, pltpu.roll(plane, 1, 1))

    return (centre, zz, xx, zx, up(yy), up(-zy), up(-xy), down(yy), down(zy), down(xy))


def store_planes(planes, layer, parts, scale):
    for start in range(0, AX, 16):
        part = slice(start, start + 16)
        speed, ratio, theta, sweep = [ref[part].astype(jnp.float32) for ref in parts]
        for index, value in enumerate(weight_planes(speed * scale, ratio, theta, sweep)):
            planes[index, layer - 1, part, :] = value


def loop(first, last, body):
    def step(index, carry):
        body(index)
        return carry

    lax.fori_loop(first, last, step, 0)


def advance(source, target, planes, layer, start):
    part = slice(start, start + ROWS)
    (centre_w, zz, xx, zx, y_low, zy_low, xy_low, y_high, zy_high, xy_high) = [
        planes[i, layer - 1, part, :] for i in range(10)
    ]
    here = slice(PAD + start, PAD + start + ROWS)
    before = slice(PAD + start - 1, PAD + start + ROWS - 1)
    after = slice(PAD + start + 1, PAD + start + ROWS + 1)
    made = []
    for field in range(2):
        centre = source[field, layer, here, :]
        above = source[field, layer + 1, here, :]
        below = source[field, layer - 1, here, :]
        ahead = source[field, layer, after, :]
        behind = source[field, layer, before, :]
        step_z = above - below
        step_x = ahead - behind
        twist = (source[field, layer + 1, after, :] - source[field, layer + 1, before, :]) - (
            source[field, layer - 1, after, :] - source[field, layer - 1, before, :]
        )
        total = centre_w * centre - target[field, layer, here, :]
        total = total + zz * (above + below)
        total = total + xx * (ahead + behind)
        total = total + zx * twist
        total = total + pltpu.roll(y_low * centre + zy_low * step_z + xy_low * step_x, 1, 1)
        total = total + pltpu.roll(y_high * centre + zy_high * step_z + xy_high * step_x, AY - 1, 1)
        target[field, layer, here, :] = total
        made.append(total)
    return made


def advance_halo(source, target, planes, first, last):
    def halo(layer):
        for start in range(0, AX, ROWS):
            advance(source, target, planes, layer, start)

    if last > first:
        loop(first, last, halo)


def advance_own(source, target, planes, picture, fresh):
    def own(layer):
        for start in range(0, AX, ROWS):
            made = advance(source, target, planes, layer + W, start)
            place = pl.ds(pl.multiple_of(layer * AX + start, ROWS), ROWS)
            product = made[0] * made[1]
            picture[place, :] = product if fresh else picture[place, :] + product

    loop(0, SLAB, own)


def own_kernel(cur, prev, speed, ratio, tilt, azimuth, jump, column_scale, first, second, planes, inverse, stack):
    zeros = jnp.zeros((PAD, AY), jnp.float32)

    def clear(layer):
        for field in range(2):
            for buffer in (first, second):
                buffer[field, layer, 0:PAD, :] = zeros
                buffer[field, layer, PAD + AX : PAD + AX + PAD, :] = zeros

    def fill(layer):
        for field in range(2):
            first[field, layer + W, BODY, :] = cur[field, layer]
            second[field, layer + W, BODY, :] = prev[field, layer]
        store_planes(planes, layer + W, [ref.at[layer] for ref in (speed, ratio, tilt, azimuth)], 1.0)

    loop(0, EXT, clear)
    loop(0, SLAB, fill)
    invert(jump, column_scale, inverse, stack)


def take_halo(edge, fields_low, media_low, fields_high, media_high, first, second, planes, count, base_low, base_high):
    scales = (edge[0], edge[1])
    others = media_low.shape[1]
    for fields, media, scale, base, later in (
        (fields_low, media_low, scales[0], base_low, base_low + 1),
        (fields_high, media_high, scales[1], base_high, base_high - (base_high > W + SLAB)),
    ):
        def take(layer):
            for field in range(2):
                first[field, layer + base, BODY, :] = fields[field, layer] * scale

        def take_other(layer):
            for field in range(2):
                second[field, layer + later, BODY, :] = fields[field, layer + count] * scale
            store_planes(planes, layer + later, [media.at[i, layer] for i in range(4)], scale)

        loop(0, count, take)
        loop(0, others, take_other)


def near_kernel(
    edge, fields_low, media_low, fields_high, media_high, first_in, second_in, planes_in,
    first, second, planes, picture,
):
    take_halo(
        edge, fields_low, media_low, fields_high, media_high, first, second, planes, NEAR, W - NEAR, W + SLAB
    )
    for step in range(1, NEAR + 1):
        source, target = (first, second) if step % 2 else (second, first)
        advance_halo(source, target, planes, W - NEAR + step, W)
        advance_own(source, target, planes, picture, step == 1)
        advance_halo(source, target, planes, W + SLAB, W + SLAB + NEAR - step)


def far_kernel(
    edge, chosen, fields_low, media_low, fields_high, media_high, first_in, second_in, planes_in, picture_in,
    first, second, planes, picture, send,
):
    far = W - NEAR
    take_halo(
        edge, fields_low, media_low, fields_high, media_high, first, second, planes, far, 0, W + SLAB + NEAR
    )
    for step in range(1, NT + 1):
        source, target = (first, second) if step % 2 else (second, first)
        if step <= NEAR:
            advance_halo(source, target, planes, step, step + far)
            advance_halo(source, target, planes, EXT - step - far, EXT - step)
            continue
        advance_halo(source, target, planes, step, W)
        advance_own(source, target, planes, picture, False)
        advance_halo(source, target, planes, W + SLAB, EXT - step)
    for entry in range(chosen.shape[0]):
        send[entry] = picture[pl.ds(chosen[entry], SLAB, stride=AX), :]


VM = pl.BlockSpec(memory_space=pltpu.VMEM)
SM = pl.BlockSpec(memory_space=pltpu.SMEM)
DOUBLINGS = 14
GRANT = 28 << 20


def invert(jump, column_scale, inverse, stack):
    size = jump.shape[0]
    row = lax.broadcasted_iota(jnp.int32, (size, size), 0)
    column = lax.broadcasted_iota(jnp.int32, (size, size), 1)
    stack[0:size, :] = (row == column).astype(jnp.float32)
    stack[size : 2 * size, :] = jump[...]

    def double(counter, carry):
        grown = lax.dot_general(
            stack[...], stack[size : 2 * size, :], (((1,), (0,)), ((), ())),
            precision=lax.Precision.HIGHEST, preferred_element_type=jnp.float32,
        )
        stack[0:size, :] = stack[0:size, :] + grown[:size]
        stack[size : 2 * size, :] = grown[size:]
        return carry

    lax.fori_loop(0, DOUBLINGS, double, 0)
    inverse[...] = stack[0:size, :] * column_scale[...]


def band_parts(band_width, depth_damp):
    length = band_width.shape[0]
    index = jnp.arange(length, dtype=jnp.int32)
    distance = jnp.abs(index[:, None] - index[None, :])
    reach = jnp.maximum(band_width[:, None], band_width[None, :])
    adjacent = ((distance > 0) & (distance <= reach)).astype(jnp.float32)
    scale = 1.0 / (depth_damp + jnp.sum(adjacent, axis=1))
    return adjacent * scale[:, None], scale[None, :]


def gather_kernel(place, rows_in, out, held):
    for slot in range(held.shape[0]):
        held[slot] = jnp.zeros((SLAB, AY), jnp.float32)
    for entry in range(rows_in.shape[0]):
        slot = place[entry]
        held[slot] = held[slot] + rows_in[entry]
    slots = held.shape[0] - 1
    part = AY // out.shape[0]
    lane = lax.broadcasted_iota(jnp.int32, (SLAB, AY), 1)
    for piece in range(out.shape[0]):
        mixed = None
        for slot in range(slots):
            moved = held[slot]
            turn = (slot * part - piece * part) % AY
            if turn:
                moved = pltpu.roll(moved, turn, 1)
            mixed = moved if mixed is None else jnp.where(lane >= slot * part, moved, mixed)
        out[piece] = mixed * (1.0 / NT)


def apply_kernel(inverse, columns, out):
    solved = lax.dot_general(
        columns[...], inverse[...], (((0,), (1,)), ((), ())),
        precision=lax.Precision.HIGHEST, preferred_element_type=jnp.float32,
    )
    slots, part = out.shape[:2]
    for slot in range(slots):
        out[slot] = solved[slot * part : (slot + 1) * part]


def pick_rows(blocks, anchors):
    row = blocks - anchors
    valid = (row >= 0) & (row < AX)
    order = jnp.cumsum(valid.astype(jnp.int32), axis=1) - 1
    return row, valid, order


def shards(
    prev_fields, cur_fields, speed_term, epsilon, tilt, azimuth,
    aperture_anchor, slot_block, band_width, depth_damp,
):
    depth = lax.axis_size("depth")
    shots = lax.axis_size("shot")
    upward = [(i, (i + 1) % depth) for i in range(depth)]
    downward = [((i + 1) % depth, i) for i in range(depth)]
    prev, cur = prev_fields[0], cur_fields[0]
    media = [speed_term[0], epsilon[0], tilt[0], azimuth[0]]

    def cut(parts, first, last):
        return jnp.stack([part[first:last] for part in parts])

    def fields(cur_first, cur_last, prev_first, prev_last):
        return jnp.concatenate([cur[:, cur_first:cur_last], prev[:, prev_first:prev_last]], axis=1)

    def exchange(up, down):
        return lax.ppermute(up, "depth", upward), lax.ppermute(down, "depth", downward)

    far = SLAB - NEAR
    near_fields = exchange(fields(far, SLAB, far + 1, SLAB), fields(0, NEAR, 0, NEAR - 1))
    near_media = exchange(cut(media, far + 1, SLAB), cut(media, 0, NEAR - 1))
    far_fields = exchange(fields(0, far, 1, far + 1), fields(NEAR, SLAB, NEAR - 1, SLAB - 1))
    far_media = exchange(cut(media, 1, far + 1), cut(media, NEAR - 1, SLAB - 1))
    my_depth = lax.axis_index("depth")
    my_shot = lax.axis_index("shot")
    edge = jnp.stack([my_depth > 0, my_depth < depth - 1]).astype(jnp.float32)

    held = slot_block.shape[0] // shots
    blocks = slot_block.reshape(shots, held)
    row, valid, order = pick_rows(blocks, aperture_anchor[my_shot])
    source = jnp.stack(
        [jnp.sum(jnp.where(valid & (order == j), row, 0), axis=1) for j in range(2)], axis=1
    ).reshape(-1)
    mine = lax.dynamic_slice_in_dim(slot_block, my_shot * held, held)
    row, valid, order = pick_rows(mine[None, :], aperture_anchor[:, None])
    slot = jnp.arange(held, dtype=jnp.int32)[None, :]
    place = jnp.stack(
        [held + jnp.sum(jnp.where(valid & (order == j), slot - held, 0), axis=1) for j in range(2)], axis=1
    ).reshape(-1)

    length = band_width.shape[0]
    buffer = jax.ShapeDtypeStruct((2, EXT, AX + 2 * PAD, AY), jnp.float32)
    plane = jax.ShapeDtypeStruct((10, EXT - 2, AX, AY), jnp.float32)
    square = jax.ShapeDtypeStruct((length, length), jnp.float32)
    image = jax.ShapeDtypeStruct((SLAB * AX, AY), jnp.float32)
    sent = jax.ShapeDtypeStruct((2 * shots, SLAB, AY), jnp.float32)
    grant = pltpu.CompilerParams(vmem_limit_bytes=GRANT)
    first, second, planes, inverse = pl.pallas_call(
        own_kernel,
        out_shape=(buffer, buffer, plane, square),
        in_specs=[VM] * 8,
        out_specs=[VM] * 4,
        scratch_shapes=[pltpu.VMEM((2 * length, length), jnp.float32)],
        compiler_params=grant,
    )(cur, prev, *media, *band_parts(band_width, depth_damp))
    first, second, planes, picture = pl.pallas_call(
        near_kernel,
        out_shape=(buffer, buffer, plane, image),
        in_specs=[SM] + [VM] * 7,
        out_specs=[VM] * 4,
        input_output_aliases={5: 0, 6: 1, 7: 2},
        compiler_params=grant,
    )(edge, near_fields[0], near_media[0], near_fields[1], near_media[1], first, second, planes)
    send = pl.pallas_call(
        far_kernel,
        out_shape=(buffer, buffer, plane, image, sent),
        in_specs=[SM, SM] + [VM] * 8,
        out_specs=[VM] * 5,
        input_output_aliases={6: 0, 7: 1, 8: 2, 9: 3},
        compiler_params=grant,
    )(edge, source, far_fields[0], far_media[0], far_fields[1], far_media[1], first, second, planes, picture)[4]
    received = lax.all_to_all(send, "shot", split_axis=0, concat_axis=0, tiled=True)
    part = AY // depth
    pieces = pl.pallas_call(
        gather_kernel,
        out_shape=jax.ShapeDtypeStruct((depth, SLAB, AY), jnp.float32),
        in_specs=[SM, VM],
        out_specs=VM,
        scratch_shapes=[pltpu.VMEM((held + 1, SLAB, AY), jnp.float32)],
        compiler_params=grant,
    )(place, received)
    columns = lax.all_to_all(pieces, "depth", split_axis=0, concat_axis=0, tiled=True)
    return pl.pallas_call(
        apply_kernel,
        out_shape=jax.ShapeDtypeStruct((held, part, AY), jnp.float32),
        in_specs=[VM, VM],
        out_specs=VM,
        compiler_params=grant,
    )(inverse, columns.reshape(AY, AY))


def solution(mesh):
    placed = (
        P("shot", None, "depth", None, None),
        P("shot", None, "depth", None, None),
        P("shot", "depth", None, None),
        P("shot", "depth", None, None),
        P("shot", "depth", None, None),
        P("shot", "depth", None, None),
        P(),
        P(),
        P(),
        P(),
    )
    return jax.shard_map(
        shards, mesh=mesh, in_specs=placed, out_specs=P("shot", "depth", None), check_vma=False
    )
```

```python
import jax
import jax.numpy as jnp
from jax import lax
from jax.experimental import pallas as pl
from jax.experimental.pallas import tpu as pltpu
from jax.sharding import PartitionSpec as P

NT = 8
W = 4
SLAB = 8
EXT = SLAB + 2 * W
AX = 64
AY = 128
PAD = 8
ROWS = 16
BODY = slice(PAD, PAD + AX)


def trig(angle):
    square = angle * angle
    sine = -1.0 / 39916800.0
    for term in (1.0 / 362880.0, -1.0 / 5040.0, 1.0 / 120.0, -1.0 / 6.0, 1.0):
        sine = sine * square + term
    cosine = 1.0 / 479001600.0
    for term in (-1.0 / 3628800.0, 1.0 / 40320.0, -1.0 / 720.0, 1.0 / 24.0, -0.5, 1.0):
        cosine = cosine * square + term
    return sine * angle, cosine


def weight_planes(speed, ratio, theta, sweep):
    sine, axis_z = trig(theta)
    half_sine, half_cosine = trig(0.5 * sweep)
    axis_x = sine * (1.0 - 2.0 * half_sine * half_sine)
    axis_y = sine * (2.0 * half_sine * half_cosine)
    tilted = -2.0 * ratio
    base = speed * (1.0 + 2.0 * ratio)
    tilted = speed * tilted
    cross = 0.5 * tilted
    zz = base + tilted * axis_z * axis_z
    xx = base + tilted * axis_x * axis_x
    yy = base + tilted * axis_y * axis_y
    zx = cross * axis_z * axis_x
    zy = cross * axis_z * axis_y
    xy = cross * axis_x * axis_y
    centre = 2.0 - 2.0 * (zz + xx + yy)
    lane = lax.broadcasted_iota(jnp.int32, speed.shape, 1)
    low = lane == 0
    high = lane == AY - 1

    def up(plane):
        return jnp.where(high, 0.0, pltpu.roll(plane, AY - 1, 1))

    def down(plane):
        return jnp.where(low, 0.0, pltpu.roll(plane, 1, 1))

    return (centre, zz, xx, zx, up(yy), up(-zy), up(-xy), down(yy), down(zy), down(xy))


def store_planes(planes, layer, parts, scale):
    for start in range(0, AX, 16):
        part = slice(start, start + 16)
        speed, ratio, theta, sweep = [ref[part].astype(jnp.float32) for ref in parts]
        for index, value in enumerate(weight_planes(speed * scale, ratio, theta, sweep)):
            planes[index, layer - 1, part, :] = value


def loop(first, last, body):
    def step(index, carry):
        body(index)
        return carry

    lax.fori_loop(first, last, step, 0)


def advance(source, target, planes, layer, start):
    part = slice(start, start + ROWS)
    (centre_w, zz, xx, zx, y_low, zy_low, xy_low, y_high, zy_high, xy_high) = [
        planes[i, layer - 1, part, :] for i in range(10)
    ]
    here = slice(PAD + start, PAD + start + ROWS)
    before = slice(PAD + start - 1, PAD + start + ROWS - 1)
    after = slice(PAD + start + 1, PAD + start + ROWS + 1)
    made = []
    for field in range(2):
        centre = source[field, layer, here, :]
        above = source[field, layer + 1, here, :]
        below = source[field, layer - 1, here, :]
        ahead = source[field, layer, after, :]
        behind = source[field, layer, before, :]
        step_z = above - below
        step_x = ahead - behind
        twist = (source[field, layer + 1, after, :] - source[field, layer + 1, before, :]) - (
            source[field, layer - 1, after, :] - source[field, layer - 1, before, :]
        )
        total = centre_w * centre - target[field, layer, here, :]
        total = total + zz * (above + below)
        total = total + xx * (ahead + behind)
        total = total + zx * twist
        total = total + pltpu.roll(y_low * centre + zy_low * step_z + xy_low * step_x, 1, 1)
        total = total + pltpu.roll(y_high * centre + zy_high * step_z + xy_high * step_x, AY - 1, 1)
        target[field, layer, here, :] = total
        made.append(total)
    return made


def advance_halo(source, target, planes, first, last):
    def halo(layer):
        for start in range(0, AX, ROWS):
            advance(source, target, planes, layer, start)

    if last > first:
        loop(first, last, halo)


def advance_own(source, target, planes, picture, fresh):
    def own(layer):
        for start in range(0, AX, ROWS):
            made = advance(source, target, planes, layer + W, start)
            place = pl.ds(pl.multiple_of(layer * AX + start, ROWS), ROWS)
            product = made[0] * made[1]
            picture[place, :] = product if fresh else picture[place, :] + product

    loop(0, SLAB, own)


def pack_kernel(cur, prev, speed, ratio, tilt, azimuth, up_fields, up_media, down_fields, down_media, sems):
    copies = []
    for field in range(2):
        copies.append((cur.at[field, SLAB - W : SLAB], up_fields.at[field, 0:W]))
        copies.append((cur.at[field, 0:W], down_fields.at[field, 0:W]))
        copies.append((prev.at[field, SLAB - W + 1 : SLAB], up_fields.at[field, W : 2 * W - 1]))
        copies.append((prev.at[field, 0 : W - 1], down_fields.at[field, W : 2 * W - 1]))
    for index, part in enumerate((speed, ratio, tilt, azimuth)):
        copies.append((part.at[SLAB - W + 1 : SLAB], up_media.at[index]))
        copies.append((part.at[0 : W - 1], down_media.at[index]))
    started = [pltpu.make_async_copy(a, b, sems.at[i]) for i, (a, b) in enumerate(copies)]
    for copy in started:
        copy.start()
    for copy in started:
        copy.wait()


def own_kernel(cur, prev, speed, ratio, tilt, azimuth, first, second, planes, media, sems):
    own = slice(W, W + SLAB)
    copies = [(part, media.at[index]) for index, part in enumerate((speed, ratio, tilt, azimuth))]
    for field in range(2):
        copies.append((cur.at[field], first.at[field, own, BODY]))
        copies.append((prev.at[field], second.at[field, own, BODY]))
    started = [pltpu.make_async_copy(a, b, sems.at[i]) for i, (a, b) in enumerate(copies)]
    for copy in started:
        copy.start()
    zeros = jnp.zeros((PAD, AY), jnp.float32)

    def clear(layer):
        for field in range(2):
            for buffer in (first, second):
                buffer[field, layer, 0:PAD, :] = zeros
                buffer[field, layer, PAD + AX : PAD + AX + PAD, :] = zeros

    loop(0, EXT, clear)
    for copy in started:
        copy.wait()
    loop(0, SLAB, lambda layer: store_planes(planes, layer + W, [media.at[i, layer] for i in range(4)], 1.0))


def edge_scales():
    place = lax.axis_index("depth")
    last = lax.axis_size("depth") - 1
    return jnp.where(place > 0, 1.0, 0.0), jnp.where(place < last, 1.0, 0.0)


def take_fields(fields, scale, first, second, base, later):
    for field in range(2):
        def take(layer):
            first[field, layer + base, BODY, :] = fields[field, layer] * scale

        def take_other(layer):
            second[field, layer + later, BODY, :] = fields[field, layer + W] * scale

        loop(0, W, take)
        loop(0, W - 1, take_other)


def take_halos(fields_low, fields_high, first, second):
    low, high = edge_scales()
    take_fields(fields_low, low, first, second, 0, 1)
    take_fields(fields_high, high, first, second, W + SLAB, W + SLAB)


def run_steps(first, second, planes, picture, fresh):
    for step in range(1, W + 1):
        source, target = (first, second) if step % 2 else (second, first)
        advance_halo(source, target, planes, step, W)
        advance_own(source, target, planes, picture, fresh and step == 1)
        advance_halo(source, target, planes, W + SLAB, EXT - step)


def early_kernel(
    fields_low, media_low, fields_high, media_high, first_in, second_in, planes_in,
    first, second, planes, picture, up_fields, down_fields,
):
    low, high = edge_scales()

    def halo_planes(layer):
        store_planes(planes, layer + 1, [media_low.at[i, layer] for i in range(4)], low)
        store_planes(planes, layer + W + SLAB, [media_high.at[i, layer] for i in range(4)], high)

    loop(0, W - 1, halo_planes)
    take_halos(fields_low, fields_high, first, second)
    run_steps(first, second, planes, picture, True)
    for field in range(2):
        def pack(layer):
            up_fields[field, layer] = first[field, layer + SLAB, BODY, :]
            down_fields[field, layer] = first[field, layer + W, BODY, :]

        def pack_other(layer):
            up_fields[field, layer + W] = second[field, layer + SLAB + 1, BODY, :]
            down_fields[field, layer + W] = second[field, layer + W, BODY, :]

        loop(0, W, pack)
        loop(0, W - 1, pack_other)


def late_kernel(
    chosen, fields_low, fields_high, first_in, second_in, planes, picture_in,
    first, second, picture, send,
):
    take_halos(fields_low, fields_high, first, second)
    run_steps(first, second, planes, picture, False)
    for entry in range(chosen.shape[0]):
        send[entry] = picture[pl.ds(chosen[entry], SLAB, stride=AX), :]


VM = pl.BlockSpec(memory_space=pltpu.VMEM)
SM = pl.BlockSpec(memory_space=pltpu.SMEM)
HB = pl.BlockSpec(memory_space=pltpu.HBM)
DOUBLINGS = 14
GRANT = 28 << 20


def table_kernel(anchors, blocks, band_width, depth_damp, chosen, place, inverse, stack):
    size = inverse.shape[0]
    shots = anchors.shape[0]
    held = blocks.shape[0] // shots
    my_shot = lax.axis_index("shot")
    my_anchor = anchors[my_shot]

    def two_of(shot):
        taken = jnp.int32(0)
        rows = [jnp.int32(0), jnp.int32(0)]
        slots = [jnp.int32(held), jnp.int32(held)]
        sent = jnp.int32(0)
        for slot in range(held):
            row = blocks[shot * held + slot] - my_anchor
            valid = (row >= 0) & (row < AX)
            for j in range(2):
                rows[j] = jnp.where(valid & (sent == j), row, rows[j])
            sent = sent + valid.astype(jnp.int32)
            row = blocks[my_shot * held + slot] - anchors[shot]
            valid = (row >= 0) & (row < AX)
            for j in range(2):
                slots[j] = jnp.where(valid & (taken == j), slot, slots[j])
            taken = taken + valid.astype(jnp.int32)
        for j in range(2):
            chosen[2 * shot + j] = rows[j]
            place[2 * shot + j] = slots[j]

    loop(0, shots, two_of)

    row = lax.broadcasted_iota(jnp.int32, (size, size), 0)
    column = lax.broadcasted_iota(jnp.int32, (size, size), 1)
    width_row = jnp.broadcast_to(band_width[...].astype(jnp.float32), (size, size))
    reach = jnp.maximum(width_row, width_row.T)
    distance = jnp.abs(row - column).astype(jnp.float32)
    adjacent = jnp.where((distance > 0.0) & (distance <= reach), 1.0, 0.0)
    scale_row = 1.0 / (depth_damp[...] + jnp.sum(adjacent, axis=0, keepdims=True))
    stack[0:size, :] = jnp.where(row == column, 1.0, 0.0)
    stack[size : 2 * size, :] = adjacent * jnp.broadcast_to(scale_row, (size, size)).T

    def double(counter):
        grown = lax.dot_general(
            stack[...], stack[size : 2 * size, :], (((1,), (0,)), ((), ())),
            precision=lax.Precision.HIGHEST, preferred_element_type=jnp.float32,
        )
        stack[0:size, :] = stack[0:size, :] + grown[:size]
        stack[size : 2 * size, :] = grown[size:]

    loop(0, DOUBLINGS, double)
    inverse[...] = stack[0:size, :] * scale_row


def gather_kernel(place, rows_in, out, held):
    for slot in range(held.shape[0]):
        held[slot] = jnp.zeros((SLAB, AY), jnp.float32)
    for entry in range(rows_in.shape[0]):
        slot = place[entry]
        held[slot] = held[slot] + rows_in[entry]
    slots = held.shape[0] - 1
    part = AY // out.shape[0]
    lane = lax.broadcasted_iota(jnp.int32, (SLAB, AY), 1)
    for piece in range(out.shape[0]):
        mixed = None
        for slot in range(slots):
            moved = held[slot]
            turn = (slot * part - piece * part) % AY
            if turn:
                moved = pltpu.roll(moved, turn, 1)
            mixed = moved if mixed is None else jnp.where(lane >= slot * part, moved, mixed)
        out[piece] = mixed * (1.0 / NT)


def apply_kernel(inverse, columns, out):
    solved = lax.dot_general(
        columns[...], inverse[...], (((0,), (1,)), ((), ())),
        precision=lax.Precision.HIGHEST, preferred_element_type=jnp.float32,
    )
    slots, part = out.shape[:2]
    for slot in range(slots):
        out[slot] = solved[slot * part : (slot + 1) * part]


def shards(
    prev_fields, cur_fields, speed_term, epsilon, tilt, azimuth,
    aperture_anchor, slot_block, band_width, depth_damp,
):
    depth = lax.axis_size("depth")
    shots = lax.axis_size("shot")
    held = slot_block.shape[0] // shots
    length = band_width.shape[0]
    upward = [(i, (i + 1) % depth) for i in range(depth)]
    downward = [((i + 1) % depth, i) for i in range(depth)]
    prev, cur = prev_fields[0], cur_fields[0]
    media = [speed_term[0], epsilon[0], tilt[0], azimuth[0]]
    prev, cur, *media = [pltpu.with_memory_space_constraint(x, pltpu.HBM) for x in (prev, cur, *media)]

    def exchange(up, down):
        return lax.ppermute(up, "depth", upward), lax.ppermute(down, "depth", downward)

    def f32(*shape):
        return jax.ShapeDtypeStruct(shape, jnp.float32)

    buffer = f32(2, EXT, AX + 2 * PAD, AY)
    plane = f32(10, EXT - 2, AX, AY)
    edge_fields = f32(2, 2 * W - 1, AX, AY)
    edge_media = jax.ShapeDtypeStruct((4, W - 1, AX, AY), speed_term.dtype)
    table = jax.ShapeDtypeStruct((2 * shots,), jnp.int32)
    grant = pltpu.CompilerParams(vmem_limit_bytes=GRANT)
    up_fields, up_media, down_fields, down_media = pl.pallas_call(
        pack_kernel,
        out_shape=(edge_fields, edge_media, edge_fields, edge_media),
        in_specs=[HB] * 6,
        out_specs=[VM] * 4,
        scratch_shapes=[pltpu.SemaphoreType.DMA((16,))],
        compiler_params=grant,
    )(cur, prev, *media)
    fields_low, fields_high = exchange(up_fields, down_fields)
    media_low, media_high = exchange(up_media, down_media)
    first, second, planes = pl.pallas_call(
        own_kernel,
        out_shape=(buffer, buffer, plane),
        in_specs=[HB] * 6,
        out_specs=[VM] * 3,
        scratch_shapes=[
            pltpu.VMEM((4, SLAB, AX, AY), speed_term.dtype),
            pltpu.SemaphoreType.DMA((8,)),
        ],
        compiler_params=grant,
    )(cur, prev, *media)
    first, second, planes, picture, up_fields, down_fields = pl.pallas_call(
        early_kernel,
        out_shape=(buffer, buffer, plane, f32(SLAB * AX, AY), edge_fields, edge_fields),
        in_specs=[VM] * 7,
        out_specs=[VM] * 6,
        input_output_aliases={4: 0, 5: 1, 6: 2},
        compiler_params=grant,
    )(fields_low, media_low, fields_high, media_high, first, second, planes)
    up_fields, band_row = lax.optimization_barrier((up_fields, band_width[None, :]))
    fields_low, fields_high = exchange(up_fields, down_fields)
    chosen, place, inverse = pl.pallas_call(
        table_kernel,
        out_shape=(table, table, f32(length, length)),
        in_specs=[SM, SM, VM, VM],
        out_specs=[SM, SM, VM],
        scratch_shapes=[pltpu.VMEM((2 * length, length), jnp.float32)],
        compiler_params=grant,
    )(aperture_anchor, slot_block, band_row, depth_damp[None, :])
    send = pl.pallas_call(
        late_kernel,
        out_shape=(buffer, buffer, f32(SLAB * AX, AY), f32(2 * shots, SLAB, AY)),
        in_specs=[SM] + [VM] * 6,
        out_specs=[VM] * 4,
        input_output_aliases={3: 0, 4: 1, 6: 2},
        compiler_params=grant,
    )(chosen, fields_low, fields_high, first, second, planes, picture)[3]
    received = lax.all_to_all(send, "shot", split_axis=0, concat_axis=0, tiled=True)
    part = AY // depth
    pieces = pl.pallas_call(
        gather_kernel,
        out_shape=jax.ShapeDtypeStruct((depth, SLAB, AY), jnp.float32),
        in_specs=[SM, VM],
        out_specs=VM,
        scratch_shapes=[pltpu.VMEM((held + 1, SLAB, AY), jnp.float32)],
        compiler_params=grant,
    )(place, received)
    columns = lax.all_to_all(pieces, "depth", split_axis=0, concat_axis=0, tiled=True)
    return pl.pallas_call(
        apply_kernel,
        out_shape=jax.ShapeDtypeStruct((held, part, AY), jnp.float32),
        in_specs=[VM, VM],
        out_specs=VM,
        compiler_params=grant,
    )(inverse, columns.reshape(AY, AY))


def solution(mesh):
    placed = (
        P("shot", None, "depth", None, None),
        P("shot", None, "depth", None, None),
        P("shot", "depth", None, None),
        P("shot", "depth", None, None),
        P("shot", "depth", None, None),
        P("shot", "depth", None, None),
        P(),
        P(),
        P(),
        P(),
    )
    return jax.shard_map(
        shards, mesh=mesh, in_specs=placed, out_specs=P("shot", "depth", None), check_vma=False
    )
```

```python
import jax
import jax.numpy as jnp
from jax import lax
from jax.experimental import pallas as pl
from jax.experimental.pallas import tpu as pltpu
from jax.sharding import PartitionSpec as P

NT = 8
W = 4
SLAB = 8
EXT = SLAB + 2 * W
AX = 64
AY = 128
PAD = 8
ROWS = 16
BODY = slice(PAD, PAD + AX)


def trig(angle):
    square = angle * angle
    sine = -1.0 / 39916800.0
    for term in (1.0 / 362880.0, -1.0 / 5040.0, 1.0 / 120.0, -1.0 / 6.0, 1.0):
        sine = sine * square + term
    cosine = 1.0 / 479001600.0
    for term in (-1.0 / 3628800.0, 1.0 / 40320.0, -1.0 / 720.0, 1.0 / 24.0, -0.5, 1.0):
        cosine = cosine * square + term
    return sine * angle, cosine


def weight_planes(speed, ratio, theta, sweep):
    sine, axis_z = trig(theta)
    half_sine, half_cosine = trig(0.5 * sweep)
    axis_x = sine * (1.0 - 2.0 * half_sine * half_sine)
    axis_y = sine * (2.0 * half_sine * half_cosine)
    tilted = -2.0 * ratio
    base = speed * (1.0 + 2.0 * ratio)
    tilted = speed * tilted
    cross = 0.5 * tilted
    zz = base + tilted * axis_z * axis_z
    xx = base + tilted * axis_x * axis_x
    yy = base + tilted * axis_y * axis_y
    zx = cross * axis_z * axis_x
    zy = cross * axis_z * axis_y
    xy = cross * axis_x * axis_y
    centre = 2.0 - 2.0 * (zz + xx + yy)
    lane = lax.broadcasted_iota(jnp.int32, speed.shape, 1)
    low = lane == 0
    high = lane == AY - 1

    def up(plane):
        return jnp.where(high, 0.0, pltpu.roll(plane, AY - 1, 1))

    def down(plane):
        return jnp.where(low, 0.0, pltpu.roll(plane, 1, 1))

    return (centre, zz, xx, zx, up(yy), up(-zy), up(-xy), down(yy), down(zy), down(xy))


def store_planes(planes, layer, parts, scale):
    for start in range(0, AX, 16):
        part = slice(start, start + 16)
        speed, ratio, theta, sweep = [ref[part].astype(jnp.float32) for ref in parts]
        for index, value in enumerate(weight_planes(speed * scale, ratio, theta, sweep)):
            planes[index, layer - 1, part, :] = value


def loop(first, last, body):
    def step(index, carry):
        body(index)
        return carry

    lax.fori_loop(first, last, step, 0)


def advance(source, target, planes, layer, start):
    part = slice(start, start + ROWS)
    (centre_w, zz, xx, zx, y_low, zy_low, xy_low, y_high, zy_high, xy_high) = [
        planes[i, layer - 1, part, :] for i in range(10)
    ]
    here = slice(PAD + start, PAD + start + ROWS)
    before = slice(PAD + start - 1, PAD + start + ROWS - 1)
    after = slice(PAD + start + 1, PAD + start + ROWS + 1)
    made = []
    for field in range(2):
        centre = source[field, layer, here, :]
        above = source[field, layer + 1, here, :]
        below = source[field, layer - 1, here, :]
        ahead = source[field, layer, after, :]
        behind = source[field, layer, before, :]
        step_z = above - below
        step_x = ahead - behind
        twist = (source[field, layer + 1, after, :] - source[field, layer + 1, before, :]) - (
            source[field, layer - 1, after, :] - source[field, layer - 1, before, :]
        )
        total = centre_w * centre - target[field, layer, here, :]
        total = total + zz * (above + below)
        total = total + xx * (ahead + behind)
        total = total + zx * twist
        total = total + pltpu.roll(y_low * centre + zy_low * step_z + xy_low * step_x, 1, 1)
        total = total + pltpu.roll(y_high * centre + zy_high * step_z + xy_high * step_x, AY - 1, 1)
        target[field, layer, here, :] = total
        made.append(total)
    return made


def advance_layers(source, target, planes, picture, first_layer, last_layer):
    def at(layer, own):
        for start in range(0, AX, ROWS):
            made = advance(source, target, planes, layer, start)
            if own:
                place = pl.ds((layer - W) * AX + start, ROWS)
                picture[place, :] = picture[place, :] + made[0] * made[1]

    for layer in range(first_layer, last_layer):
        at(layer, W <= layer < W + SLAB)


def pack_kernel(cur, prev, speed, ratio, tilt, azimuth, up_fields, up_media, down_fields, down_media, sems):
    copies = []
    for field in range(2):
        copies.append((cur.at[field, SLAB - W : SLAB], up_fields.at[field, 0:W]))
        copies.append((cur.at[field, 0:W], down_fields.at[field, 0:W]))
        copies.append((prev.at[field, SLAB - W + 1 : SLAB], up_fields.at[field, W : 2 * W - 1]))
        copies.append((prev.at[field, 0 : W - 1], down_fields.at[field, W : 2 * W - 1]))
    for index, part in enumerate((speed, ratio, tilt, azimuth)):
        copies.append((part.at[SLAB - W + 1 : SLAB], up_media.at[index]))
        copies.append((part.at[0 : W - 1], down_media.at[index]))
    started = [pltpu.make_async_copy(a, b, sems.at[i]) for i, (a, b) in enumerate(copies)]
    for copy in started:
        copy.start()
    for copy in started:
        copy.wait()


def own_kernel(cur, prev, speed, ratio, tilt, azimuth, first, second, planes, picture, media, sems):
    own = slice(W, W + SLAB)
    copies = [(part, media.at[index]) for index, part in enumerate((speed, ratio, tilt, azimuth))]
    for field in range(2):
        copies.append((cur.at[field], first.at[field, own, BODY]))
        copies.append((prev.at[field], second.at[field, own, BODY]))
    started = [pltpu.make_async_copy(a, b, sems.at[i]) for i, (a, b) in enumerate(copies)]
    for copy in started:
        copy.start()
    zeros = jnp.zeros((PAD, AY), jnp.float32)

    def clear(layer):
        for field in range(2):
            for buffer in (first, second):
                buffer[field, layer, 0:PAD, :] = zeros
                buffer[field, layer, PAD + AX : PAD + AX + PAD, :] = zeros

    loop(0, EXT, clear)
    picture[...] = jnp.zeros_like(picture)
    for copy in started:
        copy.wait()
    loop(0, SLAB, lambda layer: store_planes(planes, layer + W, [media.at[i, layer] for i in range(4)], 1.0))
    inner_steps(first, second, planes, picture)


def edge_scales():
    place = lax.axis_index("depth")
    last = lax.axis_size("depth") - 1
    return jnp.where(place > 0, 1.0, 0.0), jnp.where(place < last, 1.0, 0.0)


def take_fields(fields, scale, first, second, base, later):
    for field in range(2):
        def take(layer):
            first[field, layer + base, BODY, :] = fields[field, layer] * scale

        def take_other(layer):
            second[field, layer + later, BODY, :] = fields[field, layer + W] * scale

        loop(0, W, take)
        loop(0, W - 1, take_other)


def take_halos(fields_low, fields_high, first, second):
    low, high = edge_scales()
    take_fields(fields_low, low, first, second, 0, 1)
    take_fields(fields_high, high, first, second, W + SLAB, W + SLAB)


def inner_steps(first, second, planes, picture):
    for step in range(1, W):
        source, target = (first, second) if step % 2 else (second, first)
        advance_layers(source, target, planes, picture, W + step, W + SLAB - step)


def outer_steps(first, second, planes, picture):
    for step in range(1, W + 1):
        source, target = (first, second) if step % 2 else (second, first)
        advance_layers(source, target, planes, picture, step, W + step)
        advance_layers(source, target, planes, picture, W + SLAB - step, EXT - step)


def early_kernel(
    fields_low, media_low, fields_high, media_high, first_in, second_in, planes_in, picture_in,
    first, second, planes, picture, up_fields, down_fields,
):
    low, high = edge_scales()

    def halo_planes(layer):
        store_planes(planes, layer + 1, [media_low.at[i, layer] for i in range(4)], low)
        store_planes(planes, layer + W + SLAB, [media_high.at[i, layer] for i in range(4)], high)

    loop(0, W - 1, halo_planes)
    take_halos(fields_low, fields_high, first, second)
    outer_steps(first, second, planes, picture)
    for field in range(2):
        def pack(layer):
            up_fields[field, layer] = first[field, layer + SLAB, BODY, :]
            down_fields[field, layer] = first[field, layer + W, BODY, :]

        def pack_other(layer):
            up_fields[field, layer + W] = second[field, layer + SLAB + 1, BODY, :]
            down_fields[field, layer + W] = second[field, layer + W, BODY, :]

        loop(0, W, pack)
        loop(0, W - 1, pack_other)


def between_kernel(first_in, second_in, planes, picture_in, first, second, picture):
    inner_steps(first, second, planes, picture)


def late_kernel(
    chosen, fields_low, fields_high, first_in, second_in, planes, picture_in,
    first, second, picture, send,
):
    take_halos(fields_low, fields_high, first, second)
    outer_steps(first, second, planes, picture)
    for entry in range(chosen.shape[0]):
        send[entry] = picture[pl.ds(chosen[entry], SLAB, stride=AX), :]


VM = pl.BlockSpec(memory_space=pltpu.VMEM)
SM = pl.BlockSpec(memory_space=pltpu.SMEM)
HB = pl.BlockSpec(memory_space=pltpu.HBM)
DOUBLINGS = 13
GRANT = 28 << 20


def table_kernel(anchors, blocks, band_width, depth_damp, chosen, place, inverse, stack):
    size = inverse.shape[0]
    shots = anchors.shape[0]
    held = blocks.shape[0] // shots
    my_shot = lax.axis_index("shot")
    my_anchor = anchors[my_shot]

    def two_of(shot):
        taken = jnp.int32(0)
        rows = [jnp.int32(0), jnp.int32(0)]
        slots = [jnp.int32(held), jnp.int32(held)]
        sent = jnp.int32(0)
        for slot in range(held):
            row = blocks[shot * held + slot] - my_anchor
            valid = (row >= 0) & (row < AX)
            for j in range(2):
                rows[j] = jnp.where(valid & (sent == j), row, rows[j])
            sent = sent + valid.astype(jnp.int32)
            row = blocks[my_shot * held + slot] - anchors[shot]
            valid = (row >= 0) & (row < AX)
            for j in range(2):
                slots[j] = jnp.where(valid & (taken == j), slot, slots[j])
            taken = taken + valid.astype(jnp.int32)
        for j in range(2):
            chosen[2 * shot + j] = rows[j]
            place[2 * shot + j] = slots[j]

    loop(0, shots, two_of)

    row = lax.broadcasted_iota(jnp.int32, (size, size), 0)
    column = lax.broadcasted_iota(jnp.int32, (size, size), 1)
    width_row = jnp.broadcast_to(band_width[...].astype(jnp.float32), (size, size))
    reach = jnp.maximum(width_row, width_row.T)
    distance = jnp.abs(row - column).astype(jnp.float32)
    adjacent = jnp.where((distance > 0.0) & (distance <= reach), 1.0, 0.0)
    scale_row = 1.0 / (depth_damp[...] + jnp.sum(adjacent, axis=0, keepdims=True))
    stack[0:size, :] = jnp.where(row == column, 1.0, 0.0)
    stack[size : 2 * size, :] = adjacent * jnp.broadcast_to(scale_row, (size, size)).T

    def double(counter):
        grown = lax.dot_general(
            stack[...], stack[size : 2 * size, :], (((1,), (0,)), ((), ())),
            precision=lax.Precision.HIGHEST, preferred_element_type=jnp.float32,
        )
        stack[0:size, :] = stack[0:size, :] + grown[:size]
        stack[size : 2 * size, :] = grown[size:]

    loop(0, DOUBLINGS, double)
    inverse[...] = stack[0:size, :] * scale_row


def gather_kernel(place, rows_in, out, held):
    for slot in range(held.shape[0]):
        held[slot] = jnp.zeros((SLAB, AY), jnp.float32)
    for entry in range(rows_in.shape[0]):
        slot = place[entry]
        held[slot] = held[slot] + rows_in[entry]
    slots = held.shape[0] - 1
    part = AY // out.shape[0]
    lane = lax.broadcasted_iota(jnp.int32, (SLAB, AY), 1)
    for piece in range(out.shape[0]):
        mixed = None
        for slot in range(slots):
            moved = held[slot]
            turn = (slot * part - piece * part) % AY
            if turn:
                moved = pltpu.roll(moved, turn, 1)
            mixed = moved if mixed is None else jnp.where(lane >= slot * part, moved, mixed)
        out[piece] = mixed * (1.0 / NT)


def apply_kernel(inverse, columns, out):
    solved = lax.dot_general(
        columns[...], inverse[...], (((0,), (1,)), ((), ())),
        precision=lax.Precision.HIGHEST, preferred_element_type=jnp.float32,
    )
    slots, part = out.shape[:2]
    for slot in range(slots):
        out[slot] = solved[slot * part : (slot + 1) * part]


def shards(
    prev_fields, cur_fields, speed_term, epsilon, tilt, azimuth,
    aperture_anchor, slot_block, band_width, depth_damp,
):
    depth = lax.axis_size("depth")
    shots = lax.axis_size("shot")
    held = slot_block.shape[0] // shots
    length = band_width.shape[0]
    upward = [(i, (i + 1) % depth) for i in range(depth)]
    downward = [((i + 1) % depth, i) for i in range(depth)]
    prev, cur = prev_fields[0], cur_fields[0]
    media = [speed_term[0], epsilon[0], tilt[0], azimuth[0]]
    prev, cur, *media = [pltpu.with_memory_space_constraint(x, pltpu.HBM) for x in (prev, cur, *media)]

    def exchange(up, down):
        return lax.ppermute(up, "depth", upward), lax.ppermute(down, "depth", downward)

    def f32(*shape):
        return jax.ShapeDtypeStruct(shape, jnp.float32)

    buffer = f32(2, EXT, AX + 2 * PAD, AY)
    plane = f32(10, EXT - 2, AX, AY)
    edge_fields = f32(2, 2 * W - 1, AX, AY)
    edge_media = jax.ShapeDtypeStruct((4, W - 1, AX, AY), speed_term.dtype)
    table = jax.ShapeDtypeStruct((2 * shots,), jnp.int32)
    grant = pltpu.CompilerParams(vmem_limit_bytes=GRANT)
    up_fields, up_media, down_fields, down_media = pl.pallas_call(
        pack_kernel,
        out_shape=(edge_fields, edge_media, edge_fields, edge_media),
        in_specs=[HB] * 6,
        out_specs=[VM] * 4,
        scratch_shapes=[pltpu.SemaphoreType.DMA((16,))],
        compiler_params=grant,
    )(cur, prev, *media)
    fields_low, fields_high = exchange(up_fields, down_fields)
    media_low, media_high = exchange(up_media, down_media)
    image = f32(SLAB * AX, AY)
    first, second, planes, picture = pl.pallas_call(
        own_kernel,
        out_shape=(buffer, buffer, plane, image),
        in_specs=[HB] * 6,
        out_specs=[VM] * 4,
        scratch_shapes=[
            pltpu.VMEM((4, SLAB, AX, AY), speed_term.dtype),
            pltpu.SemaphoreType.DMA((8,)),
        ],
        compiler_params=grant,
    )(cur, prev, *media)
    first, second, planes, picture, up_fields, down_fields = pl.pallas_call(
        early_kernel,
        out_shape=(buffer, buffer, plane, image, edge_fields, edge_fields),
        in_specs=[VM] * 8,
        out_specs=[VM] * 6,
        input_output_aliases={4: 0, 5: 1, 6: 2, 7: 3},
        compiler_params=grant,
    )(fields_low, media_low, fields_high, media_high, first, second, planes, picture)
    up_fields, band_row = lax.optimization_barrier((up_fields, band_width[None, :]))
    fields_low, fields_high = exchange(up_fields, down_fields)
    chosen, place, inverse = pl.pallas_call(
        table_kernel,
        out_shape=(table, table, f32(length, length)),
        in_specs=[SM, SM, VM, VM],
        out_specs=[SM, SM, VM],
        scratch_shapes=[pltpu.VMEM((2 * length, length), jnp.float32)],
        compiler_params=grant,
    )(aperture_anchor, slot_block, band_row, depth_damp[None, :])
    first, second, picture = pl.pallas_call(
        between_kernel,
        out_shape=(buffer, buffer, image),
        in_specs=[VM] * 4,
        out_specs=[VM] * 3,
        input_output_aliases={0: 0, 1: 1, 3: 2},
        compiler_params=grant,
    )(first, second, planes, picture)
    send = pl.pallas_call(
        late_kernel,
        out_shape=(buffer, buffer, image, f32(2 * shots, SLAB, AY)),
        in_specs=[SM] + [VM] * 6,
        out_specs=[VM] * 4,
        input_output_aliases={3: 0, 4: 1, 6: 2},
        compiler_params=grant,
    )(chosen, fields_low, fields_high, first, second, planes, picture)[3]
    received = lax.all_to_all(send, "shot", split_axis=0, concat_axis=0, tiled=True)
    part = AY // depth
    pieces = pl.pallas_call(
        gather_kernel,
        out_shape=jax.ShapeDtypeStruct((depth, SLAB, AY), jnp.float32),
        in_specs=[SM, VM],
        out_specs=VM,
        scratch_shapes=[pltpu.VMEM((held + 1, SLAB, AY), jnp.float32)],
        compiler_params=grant,
    )(place, received)
    columns = lax.all_to_all(pieces, "depth", split_axis=0, concat_axis=0, tiled=True)
    return pl.pallas_call(
        apply_kernel,
        out_shape=jax.ShapeDtypeStruct((held, part, AY), jnp.float32),
        in_specs=[VM, VM],
        out_specs=VM,
        compiler_params=grant,
    )(inverse, columns.reshape(AY, AY))


def solution(mesh):
    placed = (
        P("shot", None, "depth", None, None),
        P("shot", None, "depth", None, None),
        P("shot", "depth", None, None),
        P("shot", "depth", None, None),
        P("shot", "depth", None, None),
        P("shot", "depth", None, None),
        P(),
        P(),
        P(),
        P(),
    )
    return jax.shard_map(
        shards, mesh=mesh, in_specs=placed, out_specs=P("shot", "depth", None), check_vma=False
    )
```

```python
import functools

import jax
import jax.numpy as jnp
from jax import lax
from jax.experimental import pallas as pl
from jax.experimental.pallas import tpu as pltpu
from jax.sharding import PartitionSpec as P

NT = 8
W = 4
SLAB = 8
EXT = SLAB + 2 * W
AX = 64
AY = 128
PAD = 8
ROWS = 16
BODY = slice(PAD, PAD + AX)


def trig(angle):
    square = angle * angle
    sine = -1.0 / 39916800.0
    for term in (1.0 / 362880.0, -1.0 / 5040.0, 1.0 / 120.0, -1.0 / 6.0, 1.0):
        sine = sine * square + term
    cosine = 1.0 / 479001600.0
    for term in (-1.0 / 3628800.0, 1.0 / 40320.0, -1.0 / 720.0, 1.0 / 24.0, -0.5, 1.0):
        cosine = cosine * square + term
    return sine * angle, cosine


def weight_planes(speed, ratio, theta, sweep):
    sine, axis_z = trig(theta)
    half_sine, half_cosine = trig(0.5 * sweep)
    axis_x = sine * (1.0 - 2.0 * half_sine * half_sine)
    axis_y = sine * (2.0 * half_sine * half_cosine)
    tilted = -2.0 * ratio
    base = speed * (1.0 + 2.0 * ratio)
    tilted = speed * tilted
    cross = 0.5 * tilted
    zz = base + tilted * axis_z * axis_z
    xx = base + tilted * axis_x * axis_x
    yy = base + tilted * axis_y * axis_y
    zx = cross * axis_z * axis_x
    zy = cross * axis_z * axis_y
    xy = cross * axis_x * axis_y
    centre = 2.0 - 2.0 * (zz + xx + yy)
    lane = lax.broadcasted_iota(jnp.int32, speed.shape, 1)
    low = lane == 0
    high = lane == AY - 1

    def up(plane):
        return jnp.where(high, 0.0, pltpu.roll(plane, AY - 1, 1))

    def down(plane):
        return jnp.where(low, 0.0, pltpu.roll(plane, 1, 1))

    return (centre, zz, xx, zx, up(yy), up(-zy), up(-xy), down(yy), down(zy), down(xy))


def store_planes(planes, layer, parts, scale):
    for start in range(0, AX, 16):
        part = slice(start, start + 16)
        speed, ratio, theta, sweep = [ref[part].astype(jnp.float32) for ref in parts]
        for index, value in enumerate(weight_planes(speed * scale, ratio, theta, sweep)):
            planes[index, layer - 1, part, :] = value


def loop(first, last, body):
    def step(index, carry):
        body(index)
        return carry

    lax.fori_loop(first, last, step, 0)


def advance(source, target, planes, layer, start):
    part = slice(start, start + ROWS)
    (centre_w, zz, xx, zx, y_low, zy_low, xy_low, y_high, zy_high, xy_high) = [
        planes[i, layer - 1, part, :] for i in range(10)
    ]
    here = slice(PAD + start, PAD + start + ROWS)
    before = slice(PAD + start - 1, PAD + start + ROWS - 1)
    after = slice(PAD + start + 1, PAD + start + ROWS + 1)
    made = []
    for field in range(2):
        centre = source[field, layer, here, :]
        above = source[field, layer + 1, here, :]
        below = source[field, layer - 1, here, :]
        ahead = source[field, layer, after, :]
        behind = source[field, layer, before, :]
        step_z = above - below
        step_x = ahead - behind
        twist = (source[field, layer + 1, after, :] - source[field, layer + 1, before, :]) - (
            source[field, layer - 1, after, :] - source[field, layer - 1, before, :]
        )
        total = centre_w * centre - target[field, layer, here, :]
        total = total + zz * (above + below)
        total = total + xx * (ahead + behind)
        total = total + zx * twist
        total = total + pltpu.roll(y_low * centre + zy_low * step_z + xy_low * step_x, 1, 1)
        total = total + pltpu.roll(y_high * centre + zy_high * step_z + xy_high * step_x, AY - 1, 1)
        target[field, layer, here, :] = total
        made.append(total)
    return made


def advance_layers(source, target, planes, picture, first_layer, last_layer):
    def at(layer, own):
        for start in range(0, AX, ROWS):
            made = advance(source, target, planes, layer, start)
            if own:
                place = pl.ds((layer - W) * AX + start, ROWS)
                picture[place, :] = picture[place, :] + made[0] * made[1]

    for layer in range(first_layer, last_layer):
        at(layer, W <= layer < W + SLAB)


def pack_kernel(cur, prev, speed, ratio, tilt, azimuth, up_fields, up_media, down_fields, down_media, sems):
    copies = []
    for field in range(2):
        copies.append((cur.at[field, SLAB - W : SLAB], up_fields.at[field, 0:W]))
        copies.append((cur.at[field, 0:W], down_fields.at[field, 0:W]))
        copies.append((prev.at[field, SLAB - W + 1 : SLAB], up_fields.at[field, W : 2 * W - 1]))
        copies.append((prev.at[field, 0 : W - 1], down_fields.at[field, W : 2 * W - 1]))
    for index, part in enumerate((speed, ratio, tilt, azimuth)):
        copies.append((part.at[SLAB - W + 1 : SLAB], up_media.at[index]))
        copies.append((part.at[0 : W - 1], down_media.at[index]))
    started = [pltpu.make_async_copy(a, b, sems.at[i]) for i, (a, b) in enumerate(copies)]
    for copy in started:
        copy.start()
    for copy in started:
        copy.wait()


def own_kernel(cur, prev, speed, ratio, tilt, azimuth, first, second, planes, picture, media, sems):
    own = slice(W, W + SLAB)
    copies = [(part, media.at[index]) for index, part in enumerate((speed, ratio, tilt, azimuth))]
    for field in range(2):
        copies.append((cur.at[field], first.at[field, own, BODY]))
        copies.append((prev.at[field], second.at[field, own, BODY]))
    started = [pltpu.make_async_copy(a, b, sems.at[i]) for i, (a, b) in enumerate(copies)]
    for copy in started:
        copy.start()
    zeros = jnp.zeros((PAD, AY), jnp.float32)

    def clear(layer):
        for field in range(2):
            for buffer in (first, second):
                buffer[field, layer, 0:PAD, :] = zeros
                buffer[field, layer, PAD + AX : PAD + AX + PAD, :] = zeros

    loop(0, EXT, clear)
    picture[...] = jnp.zeros_like(picture)
    for copy in started:
        copy.wait()
    loop(0, SLAB, lambda layer: store_planes(planes, layer + W, [media.at[i, layer] for i in range(4)], 1.0))
    inner_steps(first, second, planes, picture)


def edge_scales():
    place = lax.axis_index("depth")
    last = lax.axis_size("depth") - 1
    return jnp.where(place > 0, 1.0, 0.0), jnp.where(place < last, 1.0, 0.0)


def take_fields(fields, scale, first, second, base, later):
    for field in range(2):
        def take(layer):
            first[field, layer + base, BODY, :] = fields[field, layer] * scale

        def take_other(layer):
            second[field, layer + later, BODY, :] = fields[field, layer + W] * scale

        loop(0, W, take)
        loop(0, W - 1, take_other)


def inner_steps(first, second, planes, picture):
    for step in range(1, W):
        source, target = (first, second) if step % 2 else (second, first)
        advance_layers(source, target, planes, picture, W + step, W + SLAB - step)


def side_steps(high, fields, first, second, planes, picture):
    scale = edge_scales()[high]
    if high:
        take_fields(fields, scale, first, second, W + SLAB, W + SLAB)
    else:
        take_fields(fields, scale, first, second, 0, 1)
    for step in range(1, W + 1):
        source, target = (first, second) if step % 2 else (second, first)
        low = W + SLAB - step if high else step
        advance_layers(source, target, planes, picture, low, low + W)


def early_kernel(
    high, fields, media, first_in, second_in, planes_in, picture_in,
    first, second, planes, picture, edge_fields,
):
    scale = edge_scales()[high]
    base = W + SLAB if high else 1
    loop(0, W - 1, lambda layer: store_planes(planes, layer + base, [media.at[i, layer] for i in range(4)], scale))
    side_steps(high, fields, first, second, planes, picture)
    for field in range(2):
        def pack(layer):
            edge_fields[field, layer] = first[field, layer + (SLAB if high else W), BODY, :]

        def pack_other(layer):
            edge_fields[field, layer + W] = second[field, layer + (SLAB + 1 if high else W), BODY, :]

        loop(0, W, pack)
        loop(0, W - 1, pack_other)


def between_kernel(first_in, second_in, planes, picture_in, first, second, picture):
    inner_steps(first, second, planes, picture)


def late_low_kernel(fields, first_in, second_in, planes, picture_in, first, second, picture):
    side_steps(0, fields, first, second, planes, picture)


def late_high_kernel(chosen, fields, first_in, second_in, planes, picture_in, first, second, picture, send):
    side_steps(1, fields, first, second, planes, picture)
    for entry in range(chosen.shape[0]):
        send[entry] = picture[pl.ds(chosen[entry], SLAB, stride=AX), :]


VM = pl.BlockSpec(memory_space=pltpu.VMEM)
SM = pl.BlockSpec(memory_space=pltpu.SMEM)
HB = pl.BlockSpec(memory_space=pltpu.HBM)
DOUBLINGS = 13
GRANT = 28 << 20


def table_kernel(anchors, blocks, band_width, depth_damp, chosen, place, inverse, stack):
    size = inverse.shape[0]
    shots = anchors.shape[0]
    held = blocks.shape[0] // shots
    my_shot = lax.axis_index("shot")
    my_anchor = anchors[my_shot]

    def two_of(shot):
        taken = jnp.int32(0)
        rows = [jnp.int32(0), jnp.int32(0)]
        slots = [jnp.int32(held), jnp.int32(held)]
        sent = jnp.int32(0)
        for slot in range(held):
            row = blocks[shot * held + slot] - my_anchor
            valid = (row >= 0) & (row < AX)
            for j in range(2):
                rows[j] = jnp.where(valid & (sent == j), row, rows[j])
            sent = sent + valid.astype(jnp.int32)
            row = blocks[my_shot * held + slot] - anchors[shot]
            valid = (row >= 0) & (row < AX)
            for j in range(2):
                slots[j] = jnp.where(valid & (taken == j), slot, slots[j])
            taken = taken + valid.astype(jnp.int32)
        for j in range(2):
            chosen[2 * shot + j] = rows[j]
            place[2 * shot + j] = slots[j]

    loop(0, shots, two_of)

    row = lax.broadcasted_iota(jnp.int32, (size, size), 0)
    column = lax.broadcasted_iota(jnp.int32, (size, size), 1)
    width_row = jnp.broadcast_to(band_width[...].astype(jnp.float32), (size, size))
    reach = jnp.maximum(width_row, width_row.T)
    distance = jnp.abs(row - column).astype(jnp.float32)
    adjacent = jnp.where((distance > 0.0) & (distance <= reach), 1.0, 0.0)
    scale_row = 1.0 / (depth_damp[...] + jnp.sum(adjacent, axis=0, keepdims=True))
    stack[0:size, :] = jnp.where(row == column, 1.0, 0.0)
    stack[size : 2 * size, :] = adjacent * jnp.broadcast_to(scale_row, (size, size)).T

    def double(counter):
        grown = lax.dot_general(
            stack[...], stack[size : 2 * size, :], (((1,), (0,)), ((), ())),
            precision=lax.Precision.HIGHEST, preferred_element_type=jnp.float32,
        )
        stack[0:size, :] = stack[0:size, :] + grown[:size]
        stack[size : 2 * size, :] = grown[size:]

    loop(0, DOUBLINGS, double)
    inverse[...] = stack[0:size, :] * scale_row


def gather_kernel(place, rows_in, out, held):
    for slot in range(held.shape[0]):
        held[slot] = jnp.zeros((SLAB, AY), jnp.float32)
    for entry in range(rows_in.shape[0]):
        slot = place[entry]
        held[slot] = held[slot] + rows_in[entry]
    slots = held.shape[0] - 1
    part = AY // out.shape[0]
    lane = lax.broadcasted_iota(jnp.int32, (SLAB, AY), 1)
    for piece in range(out.shape[0]):
        mixed = None
        for slot in range(slots):
            moved = held[slot]
            turn = (slot * part - piece * part) % AY
            if turn:
                moved = pltpu.roll(moved, turn, 1)
            mixed = moved if mixed is None else jnp.where(lane >= slot * part, moved, mixed)
        out[piece] = mixed * (1.0 / NT)


def apply_kernel(inverse, columns, out):
    solved = lax.dot_general(
        columns[...], inverse[...], (((0,), (1,)), ((), ())),
        precision=lax.Precision.HIGHEST, preferred_element_type=jnp.float32,
    )
    slots, part = out.shape[:2]
    for slot in range(slots):
        out[slot] = solved[slot * part : (slot + 1) * part]


def shards(
    prev_fields, cur_fields, speed_term, epsilon, tilt, azimuth,
    aperture_anchor, slot_block, band_width, depth_damp,
):
    depth = lax.axis_size("depth")
    shots = lax.axis_size("shot")
    held = slot_block.shape[0] // shots
    length = band_width.shape[0]
    upward = [(i, (i + 1) % depth) for i in range(depth)]
    downward = [((i + 1) % depth, i) for i in range(depth)]
    prev, cur = prev_fields[0], cur_fields[0]
    media = [speed_term[0], epsilon[0], tilt[0], azimuth[0]]
    prev, cur, *media = [pltpu.with_memory_space_constraint(x, pltpu.HBM) for x in (prev, cur, *media)]

    def exchange(up, down):
        return lax.ppermute(up, "depth", upward), lax.ppermute(down, "depth", downward)

    def f32(*shape):
        return jax.ShapeDtypeStruct(shape, jnp.float32)

    buffer = f32(2, EXT, AX + 2 * PAD, AY)
    plane = f32(10, EXT - 2, AX, AY)
    edge_fields = f32(2, 2 * W - 1, AX, AY)
    edge_media = jax.ShapeDtypeStruct((4, W - 1, AX, AY), speed_term.dtype)
    table = jax.ShapeDtypeStruct((2 * shots,), jnp.int32)
    grant = pltpu.CompilerParams(vmem_limit_bytes=GRANT)
    up_fields, up_media, down_fields, down_media = pl.pallas_call(
        pack_kernel,
        out_shape=(edge_fields, edge_media, edge_fields, edge_media),
        in_specs=[HB] * 6,
        out_specs=[VM] * 4,
        scratch_shapes=[pltpu.SemaphoreType.DMA((16,))],
        compiler_params=grant,
    )(cur, prev, *media)
    fields_low, fields_high = exchange(up_fields, down_fields)
    media_low, media_high = exchange(up_media, down_media)
    image = f32(SLAB * AX, AY)
    first, second, planes, picture = pl.pallas_call(
        own_kernel,
        out_shape=(buffer, buffer, plane, image),
        in_specs=[HB] * 6,
        out_specs=[VM] * 4,
        scratch_shapes=[
            pltpu.VMEM((4, SLAB, AX, AY), speed_term.dtype),
            pltpu.SemaphoreType.DMA((8,)),
        ],
        compiler_params=grant,
    )(cur, prev, *media)
    def early(high, fields, media, *state):
        return pl.pallas_call(
            functools.partial(early_kernel, high),
            out_shape=(buffer, buffer, plane, image, edge_fields),
            in_specs=[VM] * 6,
            out_specs=[VM] * 5,
            input_output_aliases={2: 0, 3: 1, 4: 2, 5: 3},
            compiler_params=grant,
        )(fields, media, *state)

    *state, down_fields = early(0, fields_low, media_low, first, second, planes, picture)
    next_high = lax.ppermute(down_fields, "depth", downward)
    first, second, planes, picture, up_fields = early(1, fields_high, media_high, *state)
    up_fields, band_row = lax.optimization_barrier((up_fields, band_width[None, :]))
    next_low = lax.ppermute(up_fields, "depth", upward)
    chosen, place, inverse = pl.pallas_call(
        table_kernel,
        out_shape=(table, table, f32(length, length)),
        in_specs=[SM, SM, VM, VM],
        out_specs=[SM, SM, VM],
        scratch_shapes=[pltpu.VMEM((2 * length, length), jnp.float32)],
        compiler_params=grant,
    )(aperture_anchor, slot_block, band_row, depth_damp[None, :])
    first, second, picture = pl.pallas_call(
        between_kernel,
        out_shape=(buffer, buffer, image),
        in_specs=[VM] * 4,
        out_specs=[VM] * 3,
        input_output_aliases={0: 0, 1: 1, 3: 2},
        compiler_params=grant,
    )(first, second, planes, picture)
    first, second, picture = pl.pallas_call(
        late_low_kernel,
        out_shape=(buffer, buffer, image),
        in_specs=[VM] * 5,
        out_specs=[VM] * 3,
        input_output_aliases={1: 0, 2: 1, 4: 2},
        compiler_params=grant,
    )(next_low, first, second, planes, picture)
    send = pl.pallas_call(
        late_high_kernel,
        out_shape=(buffer, buffer, image, f32(2 * shots, SLAB, AY)),
        in_specs=[SM] + [VM] * 5,
        out_specs=[VM] * 4,
        input_output_aliases={2: 0, 3: 1, 5: 2},
        compiler_params=grant,
    )(chosen, next_high, first, second, planes, picture)[3]
    received = lax.all_to_all(send, "shot", split_axis=0, concat_axis=0, tiled=True)
    part = AY // depth
    pieces = pl.pallas_call(
        gather_kernel,
        out_shape=jax.ShapeDtypeStruct((depth, SLAB, AY), jnp.float32),
        in_specs=[SM, VM],
        out_specs=VM,
        scratch_shapes=[pltpu.VMEM((held + 1, SLAB, AY), jnp.float32)],
        compiler_params=grant,
    )(place, received)
    columns = lax.all_to_all(pieces, "depth", split_axis=0, concat_axis=0, tiled=True)
    return pl.pallas_call(
        apply_kernel,
        out_shape=jax.ShapeDtypeStruct((held, part, AY), jnp.float32),
        in_specs=[VM, VM],
        out_specs=VM,
        compiler_params=grant,
    )(inverse, columns.reshape(AY, AY))


def solution(mesh):
    placed = (
        P("shot", None, "depth", None, None),
        P("shot", None, "depth", None, None),
        P("shot", "depth", None, None),
        P("shot", "depth", None, None),
        P("shot", "depth", None, None),
        P("shot", "depth", None, None),
        P(),
        P(),
        P(),
        P(),
    )
    return jax.shard_map(
        shards, mesh=mesh, in_specs=placed, out_specs=P("shot", "depth", None), check_vma=False
    )
```
